256 devices in a mesh: seg: 4 (over x), ctx: 64 (over y, z, core).
Axes of the slice: x: 4, y: 4, z: 8, core: 2. Of those that a mesh axis runs over, the one named last changes fastest.
Arguments:
- hidden_in: bfloat16 [32768, 1024], P(('seg', 'ctx')), may hold values from -6 to 6
- queries: bfloat16 [32768, 1024], P(('seg', 'ctx')), may hold values from -6 to 6
- key_rows: bfloat16 [32768, 1024], P(('seg', 'ctx')), may hold values from -6 to 6
- values: bfloat16 [32768, 1024], P(('seg', 'ctx')), may hold values from -6 to 6
- norm_gain: float32 [1024], replicated, may hold values from 0.5 to 1.5
- out_proj: bfloat16 [1024, 1024], replicated, may hold values from -0.1875 to 0.1875
- moe_gain: float32 [1024], replicated, may hold values from 0.5 to 1.5
- w_gate: bfloat16 [64, 1024, 896], P('ctx'), may hold values from -0.1875 to 0.1875
- w_up: bfloat16 [64, 1024, 896], P('ctx'), may hold values from -0.1875 to 0.1875
- w_down: bfloat16 [64, 896, 1024], P('ctx'), may hold values from -0.1875 to 0.1875
- expert_ids: int32 [32768, 8], P(('seg', 'ctx')), may hold values from 0 to 63, all different within a row; in each aligned block of 128 rows (0 to 127, 128 to 255, ...) at most 24 rows name the same one
- route_scale: int32 [32768, 8], P(('seg', 'ctx')), may hold values from 1 to 4095
Outputs:
- layer_out: bfloat16 [32768, 1024], P(('seg', 'ctx'))
The draws below stay inside these ranges and needn't reach their ends.
Inputs may be any that keep to these rules, and one draw needn't show every extreme that they name: `expert_ids`: each row names 8 different experts. Among the rows of one device no expert is named more than 24 times, and in every draw some device names some expert exactly 24 times.
All inputs are finite; a program needn't handle non-finite values.
Results may differ from the reference program's by a relative error of at most 0.0075.
Values may be sent and summed in bfloat16 or wider, within the bound.
A program may use at most 192 MiB of HBM per device.

```python
import math
import jax
import jax.numpy as jnp
import numpy as np
from jax import lax

HEADS = 8
HEAD = 128
D = 1024
FF = 896
TOP = 8
TOK_DEV = 128
EXPERTS = 64
TOKENS = 32768
CAP = 24


def touch_ends(values, own_key, least, high):
    extent = values.shape
    spot = [jax.random.randint(jax.random.fold_in(own_key, axis), (), 0, extent[axis]) for axis in range(len(extent))]
    values = values.at[tuple(spot)].set(least)
    longest = extent.index(max(extent))
    spot[longest] = (spot[longest] + 1) % extent[longest]
    return values.at[tuple(spot)].set(high)


def levels(own_key, dims, shards, least, top_value):
    def one(position, shards_of):
        steps = jax.random.uniform(jax.random.fold_in(jax.random.fold_in(own_key, 6), position), (shards_of,), jnp.float32, least / len(shards), top_value / len(shards))
        return jnp.repeat(jnp.exp(steps), dims[position] // shards_of).reshape((-1,) + (1,) * (len(dims) - position - 1))

    loudness = one(*shards[0])
    for cut in shards[1:]:
        loudness = loudness * one(*cut)
    return loudness


def shared_out(key, own, number, rows, amount, top, limit, lean):
    order = jax.random.permutation(key, amount)
    packed, usual = load_shares(amount, rows * top, limit, lean, True), load_shares(amount, rows * top, limit, lean, False)
    places = jnp.arange(amount)

    def named(sizes, rotation):
        used = int((sizes > 0).sum())
        fixed = max(1, used // 4)
        passed = fixed + (places - fixed + rotation * (used - fixed)) % max(1, amount - fixed)
        return jnp.zeros((amount,), jnp.int32).at[order[jnp.where(places < fixed, places, passed)]].set(jnp.asarray(sizes, jnp.int32))

    sizes = jnp.where(number % 4 == 0, named(packed, number // 4), named(usual, number - number // 4 - 1))
    mixed = jax.random.permutation(jax.random.fold_in(own, 3), amount)
    donor, sink = mixed[0:amount // 2 * 2:2], mixed[1:amount // 2 * 2:2]
    room = jnp.minimum(sizes[donor] - 1, limit - sizes[sink]) // 2
    room = jnp.where((donor == order[0]) | (sink == order[0]) | (sizes[sink] == 0), 0, jnp.maximum(room, 0))
    passed = jax.random.randint(jax.random.fold_in(own, 4), (amount // 2,), 0, 1 << 20) % (room + 1)
    sizes = sizes.at[donor].add(-passed).at[sink].add(passed)
    items = jnp.searchsorted(jnp.cumsum(sizes), jnp.arange(rows * top), side="right").astype(jnp.int32)
    grid = items.reshape(top, rows).T
    grid = grid[jax.random.permutation(jax.random.fold_in(own, 1), rows)]
    rotation = jax.random.randint(jax.random.fold_in(own, 2), (rows, 1), 0, top)
    return jnp.take_along_axis(grid, (jnp.arange(top)[None, :] + rotation) % top, axis=1)


def load_shares(amount, total, most, skew, full):
    portions = [(1 << 20) // math.isqrt(rank ** skew) + 1 for rank in range(1, amount + 1)]
    largest = most if full else min(most, max(-(-total // amount), total * portions[0] // sum(portions)))
    least = 1 if total - largest >= amount - 1 else 0
    given, rest = [largest] + [least] * (amount - 1), total - largest - least * (amount - 1)
    while rest > 0:
        candidates = [i for i in range(1, amount) if given[i] < largest] or [i for i in range(1, amount) if given[i] < most]
        mass, remaining = sum([portions[i] for i in candidates]), rest
        for i in candidates:
            extra = min(most - given[i], max(1, remaining * portions[i] // mass), rest)
            given[i] = given[i] + extra
            rest = rest - extra
    return np.array(given)


def scatter_about(own_key, shape, scale, reach, split=(), kind=jnp.bfloat16):
    array = scale * jax.random.normal(own_key, shape, jnp.float32)
    if split:
        array = array * levels(own_key, shape, split, -0.22, 0.18)
    return jnp.clip(array, -reach, reach).astype(kind)


def setup_inputs(seed: int = 0) -> dict:
    splits = jax.random.split(jax.random.key(seed), 13)
    hidden_in = scatter_about(splits[0], (TOKENS, D), 1.0, 6.0, ((0, 256),))
    queries = scatter_about(splits[1], (TOKENS, D), 1.0, 6.0, ((0, 256),))
    key_rows = scatter_about(splits[2], (TOKENS, D), 1.0, 6.0, ((0, 256),))
    values = scatter_about(splits[3], (TOKENS, D), 1.0, 6.0, ((0, 256),))
    norm_gain = jnp.clip(1.0 + 0.1 * jax.random.normal(splits[4], (D,), jnp.float32), 0.5, 1.5)
    out_proj = scatter_about(splits[5], (D, D), D ** -0.5, 0.1875)
    moe_gain = jnp.clip(1.0 + 0.1 * jax.random.normal(splits[6], (D,), jnp.float32), 0.5, 1.5)
    w_gate = scatter_about(splits[7], (EXPERTS, D, FF), D ** -0.5, 0.1875, ((0, 64),))
    w_up = scatter_about(splits[8], (EXPERTS, D, FF), D ** -0.5, 0.1875, ((0, 64),))
    w_down = scatter_about(splits[9], (EXPERTS, FF, D), FF ** -0.5, 0.1875, ((0, 64),))
    expert_ids_keys = jax.random.split(jax.random.fold_in(splits[10], 1), TOKENS // TOK_DEV)
    expert_ids_turns = jax.random.permutation(jax.random.fold_in(splits[10], 3), TOKENS // TOK_DEV)
    expert_ids = jax.vmap(lambda own, number: shared_out(jax.random.fold_in(splits[10], 2), own, number, TOK_DEV, EXPERTS, TOP, CAP, 1))(expert_ids_keys, expert_ids_turns).reshape((TOKENS, TOP))
    route_scale = touch_ends(jax.random.randint(splits[11], (TOKENS, TOP), 1, 4096), jax.random.fold_in(splits[11], 1), 1, 4095).astype(jnp.int32)
    return dict(hidden_in=hidden_in, queries=queries, key_rows=key_rows, values=values, norm_gain=norm_gain, out_proj=out_proj, moe_gain=moe_gain, w_gate=w_gate, w_up=w_up, w_down=w_down, expert_ids=expert_ids, route_scale=route_scale)


def attention_all(queries, key_rows, values):
    width = math.gcd(512, TOKENS)
    count = TOKENS // width
    q_all = queries.astype(jnp.float32).reshape(count, width, HEADS, HEAD)
    k_all = key_rows.astype(jnp.float32).reshape(count, width, HEADS, HEAD)
    v_all = values.astype(jnp.float32).reshape(count, width, HEADS, HEAD)
    causal = jnp.arange(width)[:, None] >= jnp.arange(width)[None, :]
    high = lax.Precision.HIGHEST

    def stepper(states, item):
        q_blk, k_blk, v_blk = item
        carried = jnp.einsum('thd,hde->the', q_blk, states, precision=high)
        scores = jnp.einsum('thd,shd->hts', q_blk, k_blk, precision=high)
        scores = jnp.where(causal[None, :, :], scores, jnp.zeros((), jnp.float32))
        inside = jnp.einsum('hts,she->the', scores, v_blk, precision=high)
        states = states + jnp.einsum('thd,the->hde', k_blk, v_blk, precision=high)
        return (states, carried + inside)
    start = jnp.zeros((HEADS, HEAD, HEAD), jnp.float32)
    final, outputs = lax.scan(stepper, start, (q_all, k_all, v_all))
    return outputs.reshape(TOKENS, D)

def rms_scale(rows, gain):
    mean_sq = lax.optimization_barrier(jnp.mean(rows * rows, axis=1, keepdims=True))
    return rows * lax.rsqrt(mean_sq + 1e-06) * gain[None, :]

def reference(hidden_in, queries, key_rows, values, norm_gain, out_proj, moe_gain, w_gate, w_up, w_down, expert_ids, route_scale):
    attended = attention_all(queries, key_rows, values)
    normed = rms_scale(attended, norm_gain).astype(jnp.bfloat16)
    mixed = hidden_in.astype(jnp.float32) + jnp.dot(normed, out_proj, preferred_element_type=jnp.float32)
    routed = rms_scale(mixed, moe_gain).astype(jnp.bfloat16)
    scales = route_scale.astype(jnp.float32)
    weight = (scales / lax.optimization_barrier(jnp.sum(scales, axis=1, keepdims=True))).reshape(-1)
    blocksz = 512
    flat = expert_ids.reshape(-1).astype(jnp.int32)
    npairs = flat.shape[0]
    order = jnp.argsort(flat, stable=True).astype(jnp.int32)
    counts = lax.optimization_barrier(jnp.sum((flat[:, None] == jnp.arange(EXPERTS, dtype=jnp.int32)[None, :]).astype(jnp.int32), axis=0))
    padded = (counts + blocksz - 1) // blocksz * blocksz
    pstart = jnp.cumsum(padded) - padded
    cstart = jnp.cumsum(counts) - counts
    sorted_exp = flat[order]
    ranked = jnp.arange(npairs, dtype=jnp.int32) - cstart[sorted_exp]
    dest = (pstart[sorted_exp] + ranked).astype(jnp.int32)
    nblocks = npairs // blocksz + EXPERTS
    table = jnp.full((nblocks * blocksz,), -1, jnp.int32).at[dest].set(order).reshape(nblocks, blocksz)
    pend = pstart + padded
    starts = jnp.arange(nblocks, dtype=jnp.int32) * blocksz
    owner = jnp.minimum(lax.optimization_barrier(jnp.sum((pend[None, :] <= starts[:, None]).astype(jnp.int32), axis=1)), EXPERTS - 1).astype(jnp.int32)

    def expert_step(accum, item):
        members, expert = item
        valid = members >= 0
        member = jnp.maximum(members, 0)
        token_of = member // TOP
        rows = routed[token_of].astype(jnp.float32)
        gate = jnp.dot(rows, w_gate[expert].astype(jnp.float32))
        upper = jnp.dot(rows, w_up[expert].astype(jnp.float32))
        inner = lax.optimization_barrier((jax.nn.silu(gate) * upper).astype(jnp.bfloat16)).astype(jnp.float32)
        result = lax.optimization_barrier(jnp.dot(inner, w_down[expert].astype(jnp.float32)).astype(jnp.bfloat16)).astype(jnp.float32)
        factor = jnp.where(valid, weight[member], jnp.zeros((), jnp.float32))
        accum = accum.at[token_of].add(factor[:, None] * result)
        return (accum, None)
    total, unused = lax.scan(expert_step, mixed, (table, owner))
    return total.astype(jnp.bfloat16)
```

```python
import functools

import jax
import jax.numpy as jnp
from jax import lax
from jax.experimental import pallas as pl
from jax.experimental.pallas import tpu as pltpu
from jax.sharding import Mesh
from jax.sharding import PartitionSpec as P

HEADS = 8
HEAD = 128
D = 1024
TOP = 8
NTOK = 128
SEG_CTX = ("seg", "ctx_0", "ctx_1", "ctx_2")
CTX = ("ctx_0", "ctx_1", "ctx_2")
MESH = pl.DeviceIdType.MESH
F32 = jnp.float32
BF16 = jnp.bfloat16
NX, NY, NZ, NC = 4, 4, 8, 2
PIECE = 64


def iota(shape, axis):
    return lax.broadcasted_iota(jnp.int32, shape, axis)


def dot(a, b, dims=((1,), (0,))):
    return lax.dot_general(a, b, (dims, ((), ())), preferred_element_type=F32)


def rms(rows, gain):
    mean_sq = jnp.mean(rows * rows, axis=1, keepdims=True)
    return rows * lax.rsqrt(mean_sq + 1e-06) * gain


def place():
    return tuple(lax.axis_index(a) for a in SEG_CTX)


def barrier(partners):
    sem = pltpu.get_barrier_semaphore()
    for p in partners:
        pl.semaphore_signal(sem, inc=1, device_id=p, device_id_type=MESH)
    pl.semaphore_wait(sem, len(partners))


def remote(src, dst, ssem, rsem, dev):
    return pltpu.make_async_remote_copy(
        src_ref=src, dst_ref=dst, send_sem=ssem, recv_sem=rsem, device_id=dev, device_id_type=MESH
    )


def front_kernel(
    q, k, v, hid, ngain, wo, mgain, ids, scl,
    mixed, routed, meta,
    s_out, s_in, c_out, c_in, d_out, d_in, p_out, p_in, inside,
    ss, rs, sc, rc, sd, rd, sp, rp,
):
    x, y, z, c = place()
    me = z * NC + c
    column = []
    for dz in range(NZ):
        for dc in range(NC):
            if dz or dc:
                column.append((dz * NC + dc, (lax.rem(z + dz, NZ), lax.rem(c + dc, NC))))
    ys = [(o, lax.rem(y + o, NY)) for o in range(1, NY)]
    xs = [(o, lax.rem(x + o, NX)) for o in range(1, NX)]
    barrier(
        [(x, y, zz, cc) for _, (zz, cc) in column]
        + [(x, yy, z, c) for _, yy in ys]
        + [(xx, y, z, c) for _, xx in xs]
    )

    rows = NZ * NC * 16
    eye = (iota((NTOK, NTOK), 0) == iota((NTOK, NTOK), 1)).astype(F32)
    idt = lax.dot_general(
        ids[...].astype(F32), eye, (((0,), (0,)), ((), ())),
        precision=lax.Precision.HIGHEST, preferred_element_type=F32,
    )
    sct = lax.dot_general(
        scl[...].astype(F32), eye, (((0,), (0,)), ((), ())),
        precision=lax.Precision.HIGHEST, preferred_element_type=F32,
    )
    r = iota((rows, NTOK), 0)
    owner = (lax.rem(y + r % 4, NY) * (NZ * NC) + r // 16).astype(F32)
    kind = (r % 16) // 4
    chosen = jnp.zeros((rows, NTOK), F32)
    scale = jnp.zeros((rows, NTOK), F32)
    for j in range(TOP):
        hit = owner == idt[j : j + 1, :]
        chosen = jnp.where(hit, 1.0, chosen)
        scale = jnp.where(hit, sct[j : j + 1, :], scale)
    earlier = (iota((NTOK, NTOK), 0) < iota((NTOK, NTOK), 1)).astype(BF16)
    pos = jnp.where(chosen > 0.5, dot(chosen.astype(BF16), earlier), -1.0)
    weight = scale / jnp.sum(sct, axis=0, keepdims=True)
    whi = weight.astype(BF16).astype(F32)
    table = jnp.where(kind == 0, pos, jnp.where(kind == 1, whi, jnp.where(kind == 2, weight - whi, 0.0)))
    s_out[:, PIECE:, :] = table.astype(BF16).reshape(NZ * NC, 16, NTOK)

    for h in range(HEADS):
        cols = slice(h * HEAD, (h + 1) * HEAD)
        state = dot(k[:, cols], v[:, cols], ((0,), (0,)))
        for half in range(NC):
            s_out[h * NC + half, :PIECE, :] = state[half * PIECE : (half + 1) * PIECE, :].astype(BF16)
    first = []
    for o, (zz, cc) in column:
        cp = remote(s_out.at[zz * NC + cc], s_in.at[me], ss.at[o], rs.at[o], (x, y, zz, cc))
        cp.start()
        first.append(cp)
    s_in[me] = s_out[me]

    causal = iota((NTOK, NTOK), 0) >= iota((NTOK, NTOK), 1)
    for h in range(HEADS):
        cols = slice(h * HEAD, (h + 1) * HEAD)
        scores = jnp.where(causal, dot(q[:, cols], k[:, cols], ((1,), (1,))), 0.0)
        hi = scores.astype(BF16)
        lo = (scores - hi.astype(F32)).astype(BF16)
        inside[:, cols] = dot(hi, v[:, cols]) + dot(lo, v[:, cols])

    for cp in first:
        cp.wait()
    total = jnp.zeros((PIECE, HEAD), F32)
    for i in range(NZ * NC):
        total = total + s_in[i, :PIECE, :].astype(F32)
    c_out[...] = total
    second = []
    for o, yy in ys:
        cp = remote(c_out, c_in.at[o], sc.at[o], rc.at[o], (x, yy, z, c))
        cp.start()
        second.append(cp)
    meta[...] = s_in[:, PIECE:, :]
    for cp in second:
        cp.wait()
    before = jnp.zeros((PIECE, HEAD), F32)
    whole = total
    for o in range(1, NY):
        before = before + jnp.where(y >= o, c_in[o], 0.0)
        whole = whole + c_in[o]
    d_out[...] = whole
    third = []
    for o, xx in xs:
        cp = remote(d_out, d_in.at[o], sd.at[o], rd.at[o], (xx, y, z, c))
        cp.start()
        third.append(cp)
    for cp in third:
        cp.wait()
    for o in range(1, NX):
        before = before + jnp.where(x >= o, d_in[o], 0.0)
    for i in range(NZ * NC):
        p_out[i] = before.astype(BF16)
        before = before + s_in[i, :PIECE, :].astype(F32)
    fourth = []
    for o, (zz, cc) in column:
        cp = remote(p_out.at[zz * NC + cc], p_in.at[me], sp.at[o], rp.at[o], (x, y, zz, cc))
        cp.start()
        fourth.append(cp)
    p_in[me] = p_out[me]
    for cp in fourth:
        cp.wait()

    for h in range(HEADS):
        cols = slice(h * HEAD, (h + 1) * HEAD)
        state = p_in[h * NC : (h + 1) * NC].reshape(HEAD, HEAD)
        inside[:, cols] = inside[:, cols] + dot(q[:, cols], state)
    normed = rms(inside[...], ngain[...]).astype(BF16)
    for n in range(0, D, 256):
        cols = slice(n, n + 256)
        mixed[:, cols] = hid[:, cols].astype(F32) + dot(normed, wo[:, cols])
    routed[...] = rms(mixed[...], mgain[...]).astype(BF16)


def front(q, k, v, hid, ngain, wo, mgain, ids, scl):
    sem = pltpu.SemaphoreType.DMA
    vmem = pl.BlockSpec(memory_space=pltpu.VMEM)
    col = NZ * NC
    return pl.pallas_call(
        front_kernel,
        out_shape=(
            jax.ShapeDtypeStruct((NTOK, D), F32),
            jax.ShapeDtypeStruct((NTOK, D), BF16),
            jax.ShapeDtypeStruct((col, 16, NTOK), BF16),
        ),
        in_specs=[vmem] * 9,
        out_specs=(vmem, vmem, vmem),
        scratch_shapes=[
            pltpu.VMEM((col, PIECE + 16, HEAD), BF16),
            pltpu.VMEM((col, PIECE + 16, HEAD), BF16),
            pltpu.VMEM((PIECE, HEAD), F32),
            pltpu.VMEM((NY, PIECE, HEAD), F32),
            pltpu.VMEM((PIECE, HEAD), F32),
            pltpu.VMEM((NX, PIECE, HEAD), F32),
            pltpu.VMEM((col, PIECE, HEAD), BF16),
            pltpu.VMEM((col, PIECE, HEAD), BF16),
            pltpu.VMEM((NTOK, D), F32),
            sem((col,)), sem((col,)), sem((NY,)), sem((NY,)),
            sem((NX,)), sem((NX,)), sem((col,)), sem((col,)),
        ],
        compiler_params=pltpu.CompilerParams(collective_id=0, has_side_effects=True),
    )(q, k, v, hid, ngain, wo, mgain, ids, scl)


def expert_rows(arrived, w_gate, w_up, w_down):
    sources, slots = (arrived.shape[0], arrived.shape[1])
    rows = arrived.reshape(sources * slots, D)
    gate = jnp.dot(rows, w_gate[0], preferred_element_type=jnp.float32)
    upper = jnp.dot(rows, w_up[0], preferred_element_type=jnp.float32)
    inner = (jax.nn.silu(gate) * upper).astype(jnp.bfloat16)
    result = jnp.dot(inner, w_down[0], preferred_element_type=jnp.float32).astype(jnp.bfloat16)
    return result.reshape(sources, slots, D)


def body(
    hidden_in, queries, key_rows, values, norm_gain, out_proj, moe_gain,
    w_gate, w_up, w_down, expert_ids, route_scale,
):
    ntok = queries.shape[0]
    high = lax.Precision.HIGHEST
    mixed, routed, _ = front(
        queries, key_rows, values, hidden_in, norm_gain[None, :], out_proj, moe_gain[None, :],
        expert_ids, route_scale,
    )
    experts_all = lax.axis_size(CTX) * w_gate.shape[0]
    capacity = min(ntok, 3 * ntok * TOP // (2 * experts_all))
    expert_grid = jnp.arange(experts_all, dtype=jnp.int32)
    chosen = (expert_ids[:, :, None] == expert_grid[None, None, :]).astype(jnp.float32)
    per_token = jnp.sum(chosen, axis=1)
    lower = (jnp.arange(ntok)[:, None] > jnp.arange(ntok)[None, :]).astype(jnp.float32)
    before_tok = jnp.dot(lower, per_token, precision=high)
    position = jnp.sum(chosen * before_tok[:, None, :], axis=2).astype(jnp.int32)
    slot_id = expert_ids * capacity + position
    slot_grid = jnp.arange(experts_all * capacity, dtype=jnp.int32)
    placing = jnp.sum(
        (slot_id[:, :, None] == slot_grid[None, None, :]).astype(jnp.float32), axis=1
    ).astype(jnp.bfloat16)
    outgoing = jnp.einsum("ts,td->sd", placing, routed, preferred_element_type=jnp.float32)
    outgoing = outgoing.astype(jnp.bfloat16).reshape(experts_all, capacity, D)
    came_back = lax.all_to_all(
        expert_rows(
            lax.all_to_all(outgoing, CTX, split_axis=0, concat_axis=0, tiled=True),
            w_gate,
            w_up,
            w_down,
        ),
        CTX,
        split_axis=0,
        concat_axis=0,
        tiled=True,
    )
    back_rows = came_back.reshape(experts_all * capacity, D)
    picked = back_rows[slot_id.reshape(-1)].reshape(ntok, TOP, D).astype(jnp.float32)
    scales = route_scale.astype(jnp.float32)
    weight = scales / jnp.sum(scales, axis=1, keepdims=True)
    combined = jnp.sum(weight[:, :, None] * picked, axis=1)
    return (mixed + combined).astype(jnp.bfloat16)


def solution(mesh):
    finer = Mesh(
        mesh.devices.reshape(mesh.shape["seg"], 4, 8, 2), ("seg", "ctx_0", "ctx_1", "ctx_2")
    )
    placed = (
        P(SEG_CTX, None),
        P(SEG_CTX, None),
        P(SEG_CTX, None),
        P(SEG_CTX, None),
        P(),
        P(),
        P(),
        P(CTX, None, None),
        P(CTX, None, None),
        P(CTX, None, None),
        P(SEG_CTX, None),
        P(SEG_CTX, None),
    )
    return jax.shard_map(
        body, mesh=finer, in_specs=placed, out_specs=P(SEG_CTX, None), check_vma=False
    )
```

```python
import functools

import jax
import jax.numpy as jnp
from jax import lax
from jax.experimental import pallas as pl
from jax.experimental.pallas import tpu as pltpu
from jax.sharding import Mesh
from jax.sharding import PartitionSpec as P

HEADS = 8
HEAD = 128
D = 1024
TOP = 8
NTOK = 128
SEG_CTX = ("seg", "ctx_0", "ctx_1", "ctx_2")
CTX = ("ctx_0", "ctx_1", "ctx_2")
MESH = pl.DeviceIdType.MESH
F32 = jnp.float32
BF16 = jnp.bfloat16
NX, NY, NZ, NC = 4, 4, 8, 2
PIECE = 64


def iota(shape, axis):
    return lax.broadcasted_iota(jnp.int32, shape, axis)


def dot(a, b, dims=((1,), (0,))):
    return lax.dot_general(a, b, (dims, ((), ())), preferred_element_type=F32)


def rms(rows, gain):
    mean_sq = jnp.mean(rows * rows, axis=1, keepdims=True)
    return rows * lax.rsqrt(mean_sq + 1e-06) * gain


def place():
    return tuple(lax.axis_index(a) for a in SEG_CTX)


def barrier(partners):
    sem = pltpu.get_barrier_semaphore()
    for p in partners:
        pl.semaphore_signal(sem, inc=1, device_id=p, device_id_type=MESH)
    pl.semaphore_wait(sem, len(partners))


def remote(src, dst, ssem, rsem, dev):
    return pltpu.make_async_remote_copy(
        src_ref=src, dst_ref=dst, send_sem=ssem, recv_sem=rsem, device_id=dev, device_id_type=MESH
    )


def front_kernel(
    q, k, v, hid, ngain, wo, mgain, ids, scl,
    mixed, routed, meta,
    s_out, s_in, c_out, c_in, d_out, d_in, p_out, p_in, inside,
    ss, rs, sc, rc, sd, rd, sp, rp,
):
    x, y, z, c = place()
    me = z * NC + c
    column = []
    for dz in range(NZ):
        for dc in range(NC):
            if dz or dc:
                column.append((dz * NC + dc, (lax.rem(z + dz, NZ), lax.rem(c + dc, NC))))
    ys = [(o, lax.rem(y + o, NY)) for o in range(1, NY)]
    xs = [(o, lax.rem(x + o, NX)) for o in range(1, NX)]
    barrier(
        [(x, y, zz, cc) for _, (zz, cc) in column]
        + [(x, yy, z, c) for _, yy in ys]
        + [(xx, y, z, c) for _, xx in xs]
    )

    rows = NZ * NC * 16
    eye = (iota((NTOK, NTOK), 0) == iota((NTOK, NTOK), 1)).astype(F32)
    idt = lax.dot_general(
        ids[...].astype(F32), eye, (((0,), (0,)), ((), ())),
        precision=lax.Precision.HIGHEST, preferred_element_type=F32,
    )
    sct = lax.dot_general(
        scl[...].astype(F32), eye, (((0,), (0,)), ((), ())),
        precision=lax.Precision.HIGHEST, preferred_element_type=F32,
    )
    r = iota((rows, NTOK), 0)
    owner = (lax.rem(y + r % 4, NY) * (NZ * NC) + r // 16).astype(F32)
    kind = (r % 16) // 4
    chosen = jnp.zeros((rows, NTOK), F32)
    scale = jnp.zeros((rows, NTOK), F32)
    for j in range(TOP):
        hit = owner == idt[j : j + 1, :]
        chosen = jnp.where(hit, 1.0, chosen)
        scale = jnp.where(hit, sct[j : j + 1, :], scale)
    earlier = (iota((NTOK, NTOK), 0) < iota((NTOK, NTOK), 1)).astype(BF16)
    pos = jnp.where(chosen > 0.5, dot(chosen.astype(BF16), earlier), -64.0)
    weight = scale / jnp.sum(sct, axis=0, keepdims=True)
    whi = weight.astype(BF16).astype(F32)
    table = jnp.where(kind == 0, pos, jnp.where(kind == 1, whi, jnp.where(kind == 2, weight - whi, 0.0)))
    s_out[:, PIECE:, :] = table.astype(BF16).reshape(NZ * NC, 16, NTOK)

    for h in range(HEADS):
        cols = slice(h * HEAD, (h + 1) * HEAD)
        state = dot(k[:, cols], v[:, cols], ((0,), (0,)))
        for half in range(NC):
            s_out[h * NC + half, :PIECE, :] = state[half * PIECE : (half + 1) * PIECE, :].astype(BF16)
    first = []
    for o, (zz, cc) in column:
        cp = remote(s_out.at[zz * NC + cc], s_in.at[me], ss.at[o], rs.at[o], (x, y, zz, cc))
        cp.start()
        first.append(cp)
    s_in[me] = s_out[me]

    causal = iota((NTOK, NTOK), 0) >= iota((NTOK, NTOK), 1)
    for h in range(HEADS):
        cols = slice(h * HEAD, (h + 1) * HEAD)
        scores = jnp.where(causal, dot(q[:, cols], k[:, cols], ((1,), (1,))), 0.0)
        hi = scores.astype(BF16)
        lo = (scores - hi.astype(F32)).astype(BF16)
        inside[:, cols] = dot(hi, v[:, cols]) + dot(lo, v[:, cols])

    for cp in first:
        cp.wait()
    total = jnp.zeros((PIECE, HEAD), F32)
    for i in range(NZ * NC):
        total = total + s_in[i, :PIECE, :].astype(F32)
    c_out[...] = total
    second = []
    for o, yy in ys:
        cp = remote(c_out, c_in.at[o], sc.at[o], rc.at[o], (x, yy, z, c))
        cp.start()
        second.append(cp)
    meta[...] = s_in[:, PIECE:, :]
    for cp in second:
        cp.wait()
    before = jnp.zeros((PIECE, HEAD), F32)
    whole = total
    for o in range(1, NY):
        before = before + jnp.where(y >= o, c_in[o], 0.0)
        whole = whole + c_in[o]
    d_out[...] = whole
    third = []
    for o, xx in xs:
        cp = remote(d_out, d_in.at[o], sd.at[o], rd.at[o], (xx, y, z, c))
        cp.start()
        third.append(cp)
    for cp in third:
        cp.wait()
    for o in range(1, NX):
        before = before + jnp.where(x >= o, d_in[o], 0.0)
    for i in range(NZ * NC):
        p_out[i] = before.astype(BF16)
        before = before + s_in[i, :PIECE, :].astype(F32)
    fourth = []
    for o, (zz, cc) in column:
        cp = remote(p_out.at[zz * NC + cc], p_in.at[me], sp.at[o], rp.at[o], (x, y, zz, cc))
        cp.start()
        fourth.append(cp)
    p_in[me] = p_out[me]
    for cp in fourth:
        cp.wait()

    for h in range(HEADS):
        cols = slice(h * HEAD, (h + 1) * HEAD)
        state = p_in[h * NC : (h + 1) * NC].reshape(HEAD, HEAD)
        inside[:, cols] = inside[:, cols] + dot(q[:, cols], state)
    normed = rms(inside[...], ngain[...]).astype(BF16)
    for n in range(0, D, 256):
        cols = slice(n, n + 256)
        mixed[:, cols] = hid[:, cols].astype(F32) + dot(normed, wo[:, cols])
    routed[...] = rms(mixed[...], mgain[...]).astype(BF16)


def front(q, k, v, hid, ngain, wo, mgain, ids, scl):
    sem = pltpu.SemaphoreType.DMA
    vmem = pl.BlockSpec(memory_space=pltpu.VMEM)
    col = NZ * NC
    return pl.pallas_call(
        front_kernel,
        out_shape=(
            jax.ShapeDtypeStruct((NTOK, D), F32),
            jax.ShapeDtypeStruct((NTOK, D), BF16),
            jax.ShapeDtypeStruct((col, 16, NTOK), BF16),
        ),
        in_specs=[vmem] * 9,
        out_specs=(vmem, vmem, vmem),
        scratch_shapes=[
            pltpu.VMEM((col, PIECE + 16, HEAD), BF16),
            pltpu.VMEM((col, PIECE + 16, HEAD), BF16),
            pltpu.VMEM((PIECE, HEAD), F32),
            pltpu.VMEM((NY, PIECE, HEAD), F32),
            pltpu.VMEM((PIECE, HEAD), F32),
            pltpu.VMEM((NX, PIECE, HEAD), F32),
            pltpu.VMEM((col, PIECE, HEAD), BF16),
            pltpu.VMEM((col, PIECE, HEAD), BF16),
            pltpu.VMEM((NTOK, D), F32),
            sem((col,)), sem((col,)), sem((NY,)), sem((NY,)),
            sem((NX,)), sem((NX,)), sem((col,)), sem((col,)),
        ],
        compiler_params=pltpu.CompilerParams(collective_id=0, has_side_effects=True),
    )(q, k, v, hid, ngain, wo, mgain, ids, scl)


NK = NZ
SLOTS = 48
GROUP = NY * SLOTS
FF = 896


def back_kernel(
    routed, meta, mixed, wg_h, wu_h, wd_h,
    out,
    blk, pick, pick_lo, sel, rows, inner, outs, ret, pown, pb, pin, part, racc, wg, wu, wd,
    sw, sag, rag, sm, rm, sy, ry, sr, rr, sp, rp, sc, rc,
):
    x, y, z, c = place()
    right = (x, y, lax.rem(z + 1, NZ), c)
    left = (x, y, lax.rem(z + NZ - 1, NZ), c)
    mate = (x, y, z, 1 - c)
    ahead = [(x, lax.rem(y + o, NY), z, c) for o in range(NY)]
    behind = [(x, lax.rem(y + NY - o, NY), z, c) for o in range(NY)]
    loads = [
        pltpu.make_async_copy(a.at[0], b, sw.at[i])
        for i, (a, b) in enumerate(((wg_h, wg), (wu_h, wu), (wd_h, wd)))
    ]
    for cp in loads:
        cp.start()
    barrier([right, left, mate] + ahead[1:])

    def gather_copy(k, dev):
        return remote(blk.at[k, 0], blk.at[k + 2, 0], sag.at[k], rag.at[k + 2], dev)

    def half_copy(k, half, sem, dev):
        part_of = pl.ds(half * 64, 64)
        return remote(blk.at[k, 0, part_of], blk.at[7, 0, part_of], sag.at[k], rag.at[sem], dev)

    def mate_copy(k):
        return remote(blk.at[k, 0], blk.at[k, 1], sm.at[k], rm.at[k], mate)

    def arrival(k):
        return remote(routed, blk.at[k, 0], sag.at[0], rag.at[k], right)

    def own_copy(k, dev):
        return remote(routed, blk.at[k, 0], sag.at[6 + k], rag.at[k], dev)

    def out_copy(k, o):
        span = pl.ds(o * SLOTS, SLOTS)
        return remote(sel.at[k, span], rows.at[k, span], sy.at[k, o], ry.at[k, o], ahead[o])

    def back_copy(k, o):
        span = pl.ds(o * SLOTS, SLOTS)
        return remote(outs.at[k, span], ret.at[k, span], sr.at[k, o], rr.at[k, o], behind[o])

    def source(k):
        return lax.rem(z + NZ + ((k + 1) // 2) * (1 - 2 * lax.rem(k, 2)), NZ) * NC

    slot = iota((SLOTS, NTOK), 0).astype(F32)

    own_copy(1, right).start()
    own_copy(2, left).start()
    own_mate = remote(routed, blk.at[0, 1], sm.at[0], rm.at[0], mate)
    own_mate.start()
    blk[0, 0] = routed[...]

    def pass_on(k):
        @pl.when(k < 7)
        def _():
            arrival(k).wait_recv()

        @pl.when(k == 7)
        def _():
            half_copy(5, 0, 7, right).wait_recv()
            half_copy(6, 1, 8, left).wait_recv()

        @pl.when((k < 5) & (lax.rem(k, 2) == 1))
        def _():
            gather_copy(k, right).start()

        @pl.when((k < 5) & (lax.rem(k, 2) == 0))
        def _():
            gather_copy(k, left).start()

        @pl.when(k == 5)
        def _():
            half_copy(5, 0, 7, right).start()

        @pl.when(k == 6)
        def _():
            half_copy(6, 1, 8, left).start()

        mate_copy(k).start()

    def select(k):
        mate_copy(k).wait_recv()
        src = source(k)
        mine, other = meta[src + c].astype(F32), meta[src + 1 - c].astype(F32)
        mine_at, other_at = slot - (24 * c).astype(F32), slot - (24 * (1 - c)).astype(F32)
        for o in range(NY):
            span = slice(o * SLOTS, (o + 1) * SLOTS)
            pick[span, :NTOK] = (mine[o : o + 1, :] == mine_at).astype(F32).astype(BF16)
            pick[span, NTOK:] = (other[o : o + 1, :] == other_at).astype(F32).astype(BF16)
        for n in range(0, D, 256):
            cols = slice(n, n + 256)
            got = dot(pick[...], blk[k, :, :, cols].reshape(2 * NTOK, 256)).astype(BF16)
            sel[k, SLOTS:, cols] = got[SLOTS:]
            rows[k, :SLOTS, cols] = got[:SLOTS]
        for o in range(1, NY):
            out_copy(k, o).start()

    def expert(k):
        for o in range(1, NY):
            out_copy(k, o).wait_recv()
        got = rows[k]
        for n in range(0, FF, 256):
            cols = slice(n, min(FF, n + 256))
            gate, upper = dot(got, wg[:, cols]), dot(got, wu[:, cols])
            inner[:, cols] = (gate / (1.0 + jnp.exp(-gate)) * upper).astype(BF16)
        for n in range(0, D, 256):
            cols = slice(n, n + 256)
            res = dot(inner[...], wd[:, cols]).astype(BF16)
            outs[k, SLOTS:, cols] = res[SLOTS:]
            ret[k, :SLOTS, cols] = res[:SLOTS]

    def step(it, carry):
        @pl.when(it < NK)
        def _():
            select(it)

        @pl.when(it == 0)
        def _():
            pass_on(1)
            pass_on(2)
            for cp in loads:
                cp.wait()

        @pl.when(it > 0)
        def _():
            expert(it - 1)

        @pl.when((it > 0) & (it < NK - 2))
        def _():
            pass_on(it + 2)

        return carry

    lax.fori_loop(0, NK + 1, step, 0)
    for k in range(NK - 1, -1, -1):
        for o in range(1, NY):
            back_copy(k, o).start()

    def weigh(k):
        for o in range(1, NY):
            back_copy(k, o).wait_recv()
        src = source(k)
        mine, other = meta[src + c].astype(F32), meta[src + 1 - c].astype(F32)
        mine_at, other_at = slot - (24 * c).astype(F32), slot - (24 * (1 - c)).astype(F32)
        for ref, kind in ((pick, NY), (pick_lo, 2 * NY)):
            for o in range(NY):
                span = slice(o * SLOTS, (o + 1) * SLOTS)
                at = kind + o
                ref[span, :NTOK] = jnp.where(mine[o : o + 1, :] == mine_at, mine[at : at + 1, :], 0.0).astype(BF16)
                ref[span, NTOK:] = jnp.where(other[o : o + 1, :] == other_at, other[at : at + 1, :], 0.0).astype(BF16)
        for n in range(0, D, 256):
            cols = slice(n, n + 256)
            got = ret[k, :, cols]
            summed = dot(pick[...], got, ((0,), (0,))) + dot(pick_lo[...], got, ((0,), (0,)))
            pown[:, cols] = summed[:NTOK]
            pb[k, :, cols] = summed[NTOK:].astype(BF16)
        send = remote(pb.at[k], pin.at[k], sp.at[k], rp.at[k], mate)
        send.start()
        return send

    def ring_half(half):
        span = pl.ds(half * 64, 64)
        return remote(
            part.at[7, span], racc.at[5 + half, span], sc.at[7 + half], rc.at[5 + half], right if half else left
        )

    def ring_copy(k):
        to = {1: 0, 2: 7}.get(k, k - 2)
        return remote(part.at[k], racc.at[to], sc.at[k], rc.at[to], left if k % 2 else right)

    sent, mates = [], []
    for k in range(NK - 1, -1, -1):
        cp = weigh(k)
        mates.append(cp)
        cp.wait_recv()
        if k == 7:
            part[7] = (pown[...] + pin[7].astype(F32)).astype(BF16)
        elif k == 5 or k == 6:
            half = k - 5
            ring_half(half).wait_recv()
            add, keep = slice(half * 64, half * 64 + 64), slice(64 - half * 64, 128 - half * 64)
            part[k, keep] = (pown[keep] + pin[k, keep].astype(F32)).astype(BF16)
            part[k, add] = (pown[add] + pin[k, add].astype(F32) + racc[k, add].astype(F32)).astype(BF16)
        elif k:
            ring_copy(k + 2).wait_recv()
            part[k] = (pown[...] + pin[k].astype(F32) + racc[k].astype(F32)).astype(BF16)
        else:
            ring_copy(1).wait_recv()
            ring_copy(2).wait_recv()
            both = racc[0].astype(F32) + racc[7].astype(F32)
            out[...] = (mixed[...] + (pown[...] + pin[0].astype(F32) + both)).astype(BF16)
        if k:
            for cp in [ring_half(0), ring_half(1)] if k == 7 else [ring_copy(k)]:
                cp.start()
                sent.append(cp)

    own_copy(1, right).wait_send()
    own_copy(2, left).wait_send()
    for k in range(1, 5):
        gather_copy(k, right).wait_send()
    half_copy(5, 0, 7, right).wait_send()
    half_copy(6, 1, 8, left).wait_send()
    for k in range(NK):
        mate_copy(k).wait_send()
        for o in range(1, NY):
            out_copy(k, o).wait_send()
            back_copy(k, o).wait_send()
    for cp in sent + mates:
        cp.wait_send()


def back(routed, meta, mixed, w_gate, w_up, w_down):
    sem = pltpu.SemaphoreType.DMA
    vmem, away = pl.BlockSpec(memory_space=pltpu.VMEM), pl.BlockSpec(memory_space=pl.ANY)
    return pl.pallas_call(
        back_kernel,
        out_shape=jax.ShapeDtypeStruct((NTOK, D), BF16),
        in_specs=[vmem, vmem, vmem, away, away, away],
        out_specs=vmem,
        scratch_shapes=[
            pltpu.VMEM((NK, 2, NTOK, D), BF16),
            pltpu.VMEM((GROUP, 2 * NTOK), BF16),
            pltpu.VMEM((GROUP, 2 * NTOK), BF16),
            pltpu.VMEM((NK, GROUP, D), BF16),
            pltpu.VMEM((NK, GROUP, D), BF16),
            pltpu.VMEM((GROUP, FF), BF16),
            pltpu.VMEM((NK, GROUP, D), BF16),
            pltpu.VMEM((NK, GROUP, D), BF16),
            pltpu.VMEM((NTOK, D), F32),
            pltpu.VMEM((NK, NTOK, D), BF16),
            pltpu.VMEM((NK, NTOK, D), BF16),
            pltpu.VMEM((NK, NTOK, D), BF16),
            pltpu.VMEM((NK, NTOK, D), BF16),
            pltpu.VMEM((D, FF), BF16),
            pltpu.VMEM((D, FF), BF16),
            pltpu.VMEM((FF, D), BF16),
            sem((3,)), sem((9,)), sem((9,)), sem((NK,)), sem((NK,)), sem((NK, NY)), sem((NK, NY)),
            sem((NK, NY)), sem((NK, NY)), sem((NK,)), sem((NK,)), sem((9,)), sem((9,)),
        ],
        compiler_params=pltpu.CompilerParams(collective_id=1, has_side_effects=True),
    )(routed, meta, mixed, w_gate, w_up, w_down)


def body(
    hidden_in, queries, key_rows, values, norm_gain, out_proj, moe_gain,
    w_gate, w_up, w_down, expert_ids, route_scale,
):
    mixed, routed, meta = front(
        queries, key_rows, values, hidden_in, norm_gain[None, :], out_proj, moe_gain[None, :],
        expert_ids, route_scale,
    )
    return back(routed, meta, mixed, w_gate, w_up, w_down)


def solution(mesh):
    finer = Mesh(
        mesh.devices.reshape(mesh.shape["seg"], 4, 8, 2), ("seg", "ctx_0", "ctx_1", "ctx_2")
    )
    placed = (
        P(SEG_CTX, None),
        P(SEG_CTX, None),
        P(SEG_CTX, None),
        P(SEG_CTX, None),
        P(),
        P(),
        P(),
        P(CTX, None, None),
        P(CTX, None, None),
        P(CTX, None, None),
        P(SEG_CTX, None),
        P(SEG_CTX, None),
    )
    return jax.shard_map(
        body, mesh=finer, in_specs=placed, out_specs=P(SEG_CTX, None), check_vma=False
    )
```
